32 devices in a mesh: snp: 8 (over z, y), samp: 4 (over x, core).
Axes of the slice: x: 2, y: 2, z: 4, core: 2. Of those that a mesh axis runs over, the one named last changes fastest.
Arguments:
- dosage: bfloat16 [5120, 8192], P('samp', 'snp'), may hold values from 0 to 2, as said below
- observed: int32 [5120, 8192], P('samp', 'snp'), may hold values 0 or 1
- band: int32 [8], replicated, may hold values from 1 to 2
Outputs:
- linkage: float32 [8192, 5120], P(('snp', 'samp'))
The draws below stay inside these ranges and needn't reach their ends.
Inputs may be any that keep to these rules, and one draw needn't show every extreme that they name: `dosage`: real-valued dosages.
All inputs are finite; a program needn't handle non-finite values. No bound on the sum of `observed` on one device may be relied on, other than what follows from the above.
Results may differ from the reference program's by a relative error of at most 0.00055.
Values may be sent and summed in bfloat16 or wider, within the bound.
A program may use at most 128 MiB of HBM per device.

```python
import jax
import jax.numpy as jnp
from jax import lax

B = 1024
NBLK = 8
NSNP = 8192
SAMPLES = 5120


def draw_dosage(key, part):
    keys = jax.random.split(key, 10)
    count = max(B // 4, 4)
    shape = (NBLK + 2, count)
    factors = jax.random.normal(keys[0], (SAMPLES, NBLK + 2, count), jnp.float32)
    starts = (jnp.arange(NBLK + 2, dtype=jnp.int32)[:, None] - 2) * B + jax.random.randint(keys[1], shape, 0, B)
    top = (2 * B).bit_length() - 1
    exponent = jax.random.randint(keys[2], shape, 4, top)
    powers = jnp.left_shift(jnp.ones_like(exponent), exponent)
    lengths = powers + jax.random.randint(keys[3], shape, 0, 1048576) % powers
    signs = (2 * jax.random.randint(keys[4], shape, 0, 2) - 1).astype(jnp.float32)

    def one_block(blk):
        near = lax.dynamic_slice_in_dim(factors, blk, 3, 1).reshape(SAMPLES, 3 * count)
        first = lax.dynamic_slice_in_dim(starts, blk, 3, 0).reshape(3 * count)
        span = lax.dynamic_slice_in_dim(lengths, blk, 3, 0).reshape(3 * count)
        sign = lax.dynamic_slice_in_dim(signs, blk, 3, 0).reshape(3 * count)
        column = blk * B + jnp.arange(B, dtype=jnp.int32)
        cover = (first[:, None] <= column[None, :]) & (column[None, :] < first[:, None] + span[:, None])
        loads = sign[:, None] * (0.5 + 0.5 * jax.random.normal(jax.random.fold_in(keys[5], blk), (3 * count, B), jnp.float32))
        loads = jnp.where(cover, loads, 0.0)
        scale = lax.rsqrt(jnp.sum(loads * loads, axis=0) + 0.25)
        return jnp.dot(near, loads) * scale[None, :]
    latent = lax.map(one_block, jnp.arange(NBLK, dtype=jnp.int32))
    latent = jnp.transpose(latent, (1, 0, 2)).reshape(SAMPLES, NSNP)
    latent = latent + 0.6 * jax.random.normal(keys[6], (SAMPLES, NSNP), jnp.float32)
    ramp = jnp.arange(SAMPLES, dtype=jnp.float32) / SAMPLES - 0.5
    tilt = jax.random.uniform(keys[7], (NSNP,), jnp.float32, -1.5, 1.5)
    slope = jax.random.uniform(keys[8], (NSNP,), jnp.float32, 0.6, 1.6)
    offset = 0.7 * jax.random.normal(keys[9], (NSNP,), jnp.float32)
    latent = latent + ramp[:, None] * tilt[None, :]
    return (2.0 * jax.nn.sigmoid(slope * latent + offset)).astype(jnp.bfloat16)


def plant(values, own_key, smallest, top_value):
    shape = values.shape
    index_at = [jax.random.randint(jax.random.fold_in(own_key, axis), (), 0, shape[axis]) for axis in range(len(shape))]
    values = values.at[tuple(index_at)].set(smallest)
    longest = shape.index(max(shape))
    index_at[longest] = (index_at[longest] + 1) % shape[longest]
    return values.at[tuple(index_at)].set(top_value)


def setup_inputs(seed: int = 0) -> dict:
    key_of = jax.random.split(jax.random.key(seed), 4)
    dosage = draw_dosage(jax.random.fold_in(key_of[3], 71), 0)
    observed = plant((jax.random.randint(key_of[1], (SAMPLES, NSNP), 0, 10) < 9).astype(jnp.int32), jax.random.fold_in(key_of[1], 1), 0, 1)
    band = plant(jax.random.randint(key_of[2], (NBLK,), 1, 3), jax.random.fold_in(key_of[2], 1), 1, 2).astype(jnp.int32)
    return {"dosage": dosage, "observed": observed, "band": band}


eps = 1e-05

def reference(dosage, observed, band):
    weight = observed.astype(jnp.float32)
    values = dosage.astype(jnp.float32)
    cnt = lax.optimization_barrier(jnp.sum(weight, axis=0))
    first = lax.optimization_barrier(jnp.sum(weight * values, axis=0))
    second = lax.optimization_barrier(jnp.sum(weight * values * values, axis=0))
    mean = first / cnt
    spread = second - first * mean
    zed = (weight * (values - mean) * lax.rsqrt(spread + eps * cnt)).astype(jnp.bfloat16)
    padded = jnp.pad(zed, ((0, 0), (2 * B, 2 * B)))
    offsets = jnp.arange(5, dtype=jnp.int32) - 2

    def one_block(blk):
        own = lax.dynamic_slice_in_dim(zed, blk * B, B, 1)
        near = lax.dynamic_slice_in_dim(padded, blk * B, 5 * B, 1)
        gram = jnp.dot(own.T, near, preferred_element_type=jnp.float32)
        other = blk + offsets
        inside = (other >= 0) & (other < NBLK)
        other_band = band[jnp.clip(other, 0, NBLK - 1)]
        keep = inside & (jnp.abs(offsets) <= jnp.minimum(band[blk], other_band))
        keep = jnp.where(keep, 1.0, 0.0).astype(jnp.float32)
        return (gram.reshape(B, 5, B) * keep[None, :, None]).reshape(B, 5 * B)
    result = lax.map(one_block, jnp.arange(NBLK, dtype=jnp.int32))
    return result.reshape(NSNP, 5 * B)
```

```python
import functools

import jax
import jax.numpy as jnp
from jax import lax
from jax.experimental import pallas as pl
from jax.experimental.pallas import tpu as pltpu
from jax.sharding import PartitionSpec as P

eps = 1e-05
MESH = pl.DeviceIdType.MESH
CHUNK = 256


def offset_of(slot, e):
    return jnp.where(slot == 1, -e, jnp.where(slot == 2, -2 * e, jnp.where(slot == 3, 2 * e, jnp.where(slot == 4, e, 0))))


def linkage_kernel(
    nblk, nsamp, nk, band_ref, z_ref, zt_ref, out_ref,
    right, left, acc, part_out, part_in,
    local_sem, out_sem, z_send, z_recv, fwd_send, fwd_recv, relay_send, left_send, left_recv, part_send, part_recv,
):
    b = lax.axis_index("snp")
    s = lax.axis_index("samp")
    ngrp = nsamp // 2
    c = s % 2
    g = s // 2
    mate = s + 1 - 2 * c
    e = 2 * (b % 2) - 1
    width = nk * CHUNK
    nitems = 5 * nk

    def inside(block):
        return (block >= 0) & (block < nblk)

    def has(slot):
        return inside(b + offset_of(slot, e))

    def item(i):
        later = i >= nk
        j = i - nk
        return jnp.where(later, 1 + j % 4, 0), jnp.where(later, j // 4, i)

    barrier = pltpu.get_barrier_semaphore()
    peers = [(b, mate)] + [(b, 2 * ((g + j) % ngrp) + c) for j in range(1, ngrp)]
    for peer in peers:
        pl.semaphore_signal(barrier, inc=1, device_id=peer, device_id_type=MESH)
    for by in (-2, -1, 1, 2):
        @pl.when(inside(b + by))
        def _():
            pl.semaphore_signal(barrier, inc=1, device_id=(b + by, s), device_id_type=MESH)

    def load(k):
        return pltpu.make_async_copy(z_ref.at[:, pl.ds(k * CHUNK, CHUNK)], right.at[0, c, k], local_sem.at[k])

    own_left = pltpu.make_async_copy(zt_ref.at[c], left.at[c], local_sem.at[nk])
    for k in range(nk):
        load(k).start()
    own_left.start()

    beside = [jnp.where(inside(b + by), 1, 0) for by in (-2, -1, 1, 2)]
    pl.semaphore_wait(barrier, len(peers) + sum(beside))

    mate_left = pltpu.make_async_remote_copy(
        zt_ref.at[1 - c], left.at[c], left_send, left_recv, device_id=(b, mate), device_id_type=MESH)
    mate_left_in = pltpu.make_async_remote_copy(
        zt_ref.at[c], left.at[1 - c], left_send, left_recv, device_id=(b, mate), device_id_type=MESH)

    def direct(way, k):
        target = b + (-e, 2 * e, -2 * e)[way - 1]
        return target, pltpu.make_async_remote_copy(
            right.at[0, c, k], right.at[way, c, k], z_send.at[way, k], z_recv.at[way, k],
            device_id=(target, s), device_id_type=MESH)

    def relay(source, target, k):
        return pltpu.make_async_remote_copy(
            right.at[source, c, k], right.at[4, c, k], relay_send.at[k], z_recv.at[4, k],
            device_id=(target, s), device_id_type=MESH)

    def arrival(slot, k):
        return pltpu.make_async_remote_copy(
            right.at[slot, c, k], right.at[slot, c, k], z_send.at[slot, k], z_recv.at[slot, k],
            device_id=(b, mate), device_id_type=MESH)

    def forward(slot, k):
        return pltpu.make_async_remote_copy(
            right.at[slot, c, k], right.at[slot, c, k], fwd_send.at[slot, k], fwd_recv.at[slot, k],
            device_id=(b, mate), device_id_type=MESH)

    def forward_in(slot, k):
        return pltpu.make_async_remote_copy(
            right.at[slot, 1 - c, k], right.at[slot, 1 - c, k], fwd_send.at[slot, k], fwd_recv.at[slot, k],
            device_id=(b, mate), device_id_type=MESH)

    for k in range(nk):
        load(k).wait()
        if k == 0:
            mate_left.start()
        forward(0, k).start()
        for way in (1, 2, 3):
            target, copy = direct(way, k)

            @pl.when(inside(target))
            def _():
                copy.start()
    own_left.wait()

    def receive(i):
        slot, k = item(i)

        @pl.when((slot > 0) & has(slot))
        def _():
            arrival(slot, k).wait_recv()
            forward(slot, k).start()

            @pl.when((slot == 2) & (k % 2 == 0))
            def _():
                relay(2, b - e, k).start()

            @pl.when((slot == 1) & (k % 2 == 1) & has(2))
            def _():
                relay(1, b - 2 * e, k).start()

    def partial(i, j):
        return pltpu.make_async_remote_copy(
            part_out.at[i, j - 1], part_in.at[i, j - 1], part_send.at[i, j - 1], part_recv.at[i, j - 1],
            device_id=(b, 2 * ((g + j) % ngrp) + c), device_id_type=MESH)

    def multiply(i):
        slot, k = item(i)

        @pl.when(has(slot))
        def _():
            forward_in(slot, k).wait_recv()

            def rows(group):
                return jnp.dot(
                    left[0, group], right[slot, 0, k], preferred_element_type=jnp.float32
                ) + jnp.dot(left[1, group], right[slot, 1, k], preferred_element_type=jnp.float32)

            for j in range(1, ngrp):
                part_out[i, j - 1] = rows((g + j) % ngrp)
                partial(i, j).start()
            acc[i] = rows(g)

    mate_left_in.wait_recv()

    def step(i, carry):
        @pl.when(i + 1 < nitems)
        def _():
            receive(i + 1)
        multiply(i)
        return carry

    lax.fori_loop(0, nitems, step, 0)

    def store(i):
        slot, k = item(i)
        column = (offset_of(slot, e) + 2) * width + k * CHUNK
        return pltpu.make_async_copy(acc.at[i], out_ref.at[:, pl.ds(pl.multiple_of(column, CHUNK), CHUNK)], out_sem.at[i])

    def finish(i, carry):
        slot, k = item(i)

        @pl.when(has(slot))
        def _():
            total = acc[i]
            for j in range(1, ngrp):
                partial(i, j).wait_recv()
                total = total + part_in[i, j - 1]
            offset = offset_of(slot, e)
            kept = jnp.abs(offset) <= jnp.minimum(band_ref[b], band_ref[b + offset])
            acc[i] = total * jnp.where(kept, 1.0, 0.0).astype(jnp.float32)

        @pl.when(jnp.logical_not(has(slot)))
        def _():
            acc[i] = jnp.zeros(acc.shape[1:], acc.dtype)
        store(i).start()
        return carry

    lax.fori_loop(0, nitems, finish, 0)

    def drain(i, carry):
        slot, k = item(i)
        store(i).wait()

        @pl.when(has(slot))
        def _():
            forward(slot, k).wait_send()
            for j in range(1, ngrp):
                partial(i, j).wait_send()
        return carry

    lax.fori_loop(0, nitems, drain, 0)
    mate_left.wait_send()
    for k in range(nk):
        for way in (1, 2, 3):
            target, copy = direct(way, k)

            @pl.when(inside(target))
            def _():
                copy.wait_send()

        @pl.when(has(2))
        def _():
            relay(2, b - e, k).wait_send()


def linkage_of(z, zt, band, nblk, nsamp):
    depth, width = z.shape
    nk = width // CHUNK
    ngrp = nsamp // 2
    rows = width // nsamp
    nitems = 5 * nk
    dma = pltpu.SemaphoreType.DMA
    return pl.pallas_call(
        functools.partial(linkage_kernel, nblk, nsamp, nk),
        out_shape=jax.ShapeDtypeStruct((rows, 5 * width), jnp.float32),
        in_specs=[
            pl.BlockSpec(memory_space=pltpu.SMEM),
            pl.BlockSpec(memory_space=pl.ANY),
            pl.BlockSpec(memory_space=pl.ANY),
        ],
        out_specs=pl.BlockSpec(memory_space=pl.ANY),
        scratch_shapes=[
            pltpu.VMEM((5, 2, nk, depth, CHUNK), jnp.bfloat16),
            pltpu.VMEM((2, ngrp, rows, depth), jnp.bfloat16),
            pltpu.VMEM((nitems, rows, CHUNK), jnp.float32),
            pltpu.VMEM((nitems, ngrp - 1, rows, CHUNK), jnp.float32),
            pltpu.VMEM((nitems, ngrp - 1, rows, CHUNK), jnp.float32),
            dma((nk + 1,)),
            dma((nitems,)),
            dma((4, nk)),
            dma((5, nk)),
            dma((5, nk)),
            dma((5, nk)),
            dma((nk,)),
            dma,
            dma,
            dma((nitems, ngrp - 1)),
            dma((nitems, ngrp - 1)),
        ],
        compiler_params=pltpu.CompilerParams(
            collective_id=0, has_side_effects=True, vmem_limit_bytes=60 * 1024 * 1024
        ),
    )(band, z, zt)


def on_device(nblk, nsamp, dosage, observed, band):
    depth, width = dosage.shape
    weight = observed.astype(jnp.float32)
    values = dosage.astype(jnp.float32)
    cnt, first, second = lax.psum(
        (
            jnp.sum(weight, axis=0),
            jnp.sum(weight * values, axis=0),
            jnp.sum(weight * values * values, axis=0),
        ),
        "samp",
    )
    mean = first / cnt
    spread = second - first * mean
    zed = (weight * (values - mean) * lax.rsqrt(spread + eps * cnt)).astype(jnp.bfloat16)
    turned = zed.T.reshape(nsamp // 2, 2, width // nsamp, depth).transpose(1, 0, 2, 3)
    return linkage_of(zed, turned, band, nblk, nsamp)


def solution(mesh):
    return jax.shard_map(
        functools.partial(on_device, mesh.shape["snp"], mesh.shape["samp"]),
        mesh=mesh,
        in_specs=(P("samp", "snp"), P("samp", "snp"), P()),
        out_specs=P(("snp", "samp"), None),
        check_vma=False,
    )
```

```python
import functools

import jax
import jax.numpy as jnp
from jax import lax
from jax.experimental import pallas as pl
from jax.experimental.pallas import tpu as pltpu
from jax.sharding import PartitionSpec as P

eps = 1e-05
MESH = pl.DeviceIdType.MESH
CHUNK = 256


def offset_of(slot, e):
    return jnp.where(slot == 1, -e, jnp.where(slot == 2, -2 * e, jnp.where(slot == 3, 2 * e, jnp.where(slot == 4, e, 0))))


def linkage_kernel(
    nblk, nsamp, nk, band_ref, z_ref, zt_ref, out_ref,
    right, left, acc, part_out, part_in,
    local_sem, out_sem, z_send, z_recv, fwd_send, fwd_recv, relay_send, left_send, left_recv, part_send, part_recv,
):
    b = lax.axis_index("snp")
    s = lax.axis_index("samp")
    ngrp = nsamp // 2
    c = s % 2
    g = s // 2
    mate = s + 1 - 2 * c
    e = 2 * (b % 2) - 1
    width = nk * CHUNK
    nitems = 5 * nk

    def inside(block):
        return (block >= 0) & (block < nblk)

    def has(slot):
        return inside(b + offset_of(slot, e))

    def item(i):
        j = i - nk
        slot = jnp.where(i < nk, 0, jnp.where(j < 3 * nk, 1 + j % 3, 4))
        return slot, jnp.where(i < nk, i, jnp.where(j < 3 * nk, j // 3, j - 3 * nk))

    barrier = pltpu.get_barrier_semaphore()
    peers = [(b, mate)] + [(b, 2 * ((g + j) % ngrp) + c) for j in range(1, ngrp)]
    for peer in peers:
        pl.semaphore_signal(barrier, inc=1, device_id=peer, device_id_type=MESH)
    for by in (-2, -1, 1, 2):
        @pl.when(inside(b + by))
        def _():
            pl.semaphore_signal(barrier, inc=1, device_id=(b + by, s), device_id_type=MESH)

    def load(k):
        return pltpu.make_async_copy(z_ref.at[:, pl.ds(k * CHUNK, CHUNK)], right.at[0, c, k], local_sem.at[k])

    own_left = pltpu.make_async_copy(zt_ref.at[:, c], left.at[c], local_sem.at[nk])
    for k in range(nk):
        load(k).start()
    own_left.start()

    beside = [jnp.where(inside(b + by), 1, 0) for by in (-2, -1, 1, 2)]
    pl.semaphore_wait(barrier, len(peers) + sum(beside))

    mate_left = pltpu.make_async_remote_copy(
        zt_ref.at[:, 1 - c], left.at[c], left_send, left_recv, device_id=(b, mate), device_id_type=MESH)
    mate_left_in = pltpu.make_async_remote_copy(
        zt_ref.at[:, c], left.at[1 - c], left_send, left_recv, device_id=(b, mate), device_id_type=MESH)

    def direct(way, k):
        target = b + (-e, 2 * e, -2 * e)[way - 1]
        return target, pltpu.make_async_remote_copy(
            right.at[0, c, k], right.at[way, c, k], z_send.at[way, k], z_recv.at[way, k],
            device_id=(target, s), device_id_type=MESH)

    def relay(source, target, k):
        return pltpu.make_async_remote_copy(
            right.at[source, c, k], right.at[4, c, k], relay_send.at[k], z_recv.at[4, k],
            device_id=(target, s), device_id_type=MESH)

    def arrival(slot, k):
        return pltpu.make_async_remote_copy(
            right.at[slot, c, k], right.at[slot, c, k], z_send.at[slot, k], z_recv.at[slot, k],
            device_id=(b, mate), device_id_type=MESH)

    def forward(slot, k):
        return pltpu.make_async_remote_copy(
            right.at[slot, c, k], right.at[slot, c, k], fwd_send.at[slot, k], fwd_recv.at[slot, k],
            device_id=(b, mate), device_id_type=MESH)

    def forward_in(slot, k):
        return pltpu.make_async_remote_copy(
            right.at[slot, 1 - c, k], right.at[slot, 1 - c, k], fwd_send.at[slot, k], fwd_recv.at[slot, k],
            device_id=(b, mate), device_id_type=MESH)

    for k in range(nk):
        load(k).wait()
        if k == 0:
            mate_left.start()
        forward(0, k).start()
        for way in (1, 2, 3):
            target, copy = direct(way, k)

            @pl.when(inside(target))
            def _():
                copy.start()
    own_left.wait()

    def receive(i):
        slot, k = item(i)

        @pl.when((slot > 0) & has(slot))
        def _():
            arrival(slot, k).wait_recv()
            forward(slot, k).start()

            @pl.when((slot == 2) & (k % 2 == 0))
            def _():
                relay(2, b - e, k).start()

            @pl.when((slot == 1) & (k % 2 == 1) & has(2))
            def _():
                relay(1, b - 2 * e, k).start()

    def partial(i, j):
        return pltpu.make_async_remote_copy(
            part_out.at[i, j - 1], part_in.at[i, j - 1], part_send.at[i, j - 1], part_recv.at[i, j - 1],
            device_id=(b, 2 * ((g + j) % ngrp) + c), device_id_type=MESH)

    def multiply(i):
        slot, k = item(i)

        @pl.when(has(slot))
        def _():
            forward_in(slot, k).wait_recv()

            def rows(group):
                return jnp.dot(
                    left[0, group], right[slot, 0, k], preferred_element_type=jnp.float32
                ) + jnp.dot(left[1, group], right[slot, 1, k], preferred_element_type=jnp.float32)

            for j in range(1, ngrp):
                part_out[i, j - 1] = rows((g + j) % ngrp)
                partial(i, j).start()
            acc[i] = rows(g)

    mate_left_in.wait_recv()

    def step(i, carry):
        @pl.when(i + 1 < nitems)
        def _():
            receive(i + 1)
        multiply(i)
        return carry

    lax.fori_loop(0, nitems, step, 0)

    def store(i):
        slot, k = item(i)
        column = (offset_of(slot, e) + 2) * width + k * CHUNK
        return pltpu.make_async_copy(acc.at[i], out_ref.at[:, pl.ds(pl.multiple_of(column, CHUNK), CHUNK)], out_sem.at[i])

    def finish(i, carry):
        slot, k = item(i)

        @pl.when(has(slot))
        def _():
            total = acc[i]
            for j in range(1, ngrp):
                partial(i, j).wait_recv()
                total = total + part_in[i, j - 1]
            offset = offset_of(slot, e)
            kept = jnp.abs(offset) <= jnp.minimum(band_ref[b], band_ref[b + offset])
            acc[i] = total * jnp.where(kept, 1.0, 0.0).astype(jnp.float32)

        @pl.when(jnp.logical_not(has(slot)))
        def _():
            acc[i] = jnp.zeros(acc.shape[1:], acc.dtype)
        store(i).start()
        return carry

    lax.fori_loop(0, nitems, finish, 0)

    def drain(i, carry):
        slot, k = item(i)
        store(i).wait()

        @pl.when(has(slot))
        def _():
            forward(slot, k).wait_send()
            for j in range(1, ngrp):
                partial(i, j).wait_send()
        return carry

    lax.fori_loop(0, nitems, drain, 0)
    mate_left.wait_send()
    for k in range(nk):
        for way in (1, 2, 3):
            target, copy = direct(way, k)

            @pl.when(inside(target))
            def _():
                copy.wait_send()

        @pl.when(has(2))
        def _():
            relay(2, b - e, k).wait_send()


def linkage_of(z, zt, band, nblk, nsamp):
    depth, width = z.shape
    nk = width // CHUNK
    ngrp = nsamp // 2
    rows = width // nsamp
    nitems = 5 * nk
    dma = pltpu.SemaphoreType.DMA
    return pl.pallas_call(
        functools.partial(linkage_kernel, nblk, nsamp, nk),
        out_shape=jax.ShapeDtypeStruct((rows, 5 * width), jnp.float32),
        in_specs=[
            pl.BlockSpec(memory_space=pltpu.SMEM),
            pl.BlockSpec(memory_space=pl.ANY),
            pl.BlockSpec(memory_space=pl.ANY),
        ],
        out_specs=pl.BlockSpec(memory_space=pl.ANY),
        scratch_shapes=[
            pltpu.VMEM((5, 2, nk, depth, CHUNK), jnp.bfloat16),
            pltpu.VMEM((2, ngrp, rows, depth), jnp.bfloat16),
            pltpu.VMEM((nitems, rows, CHUNK), jnp.float32),
            pltpu.VMEM((nitems, ngrp - 1, rows, CHUNK), jnp.float32),
            pltpu.VMEM((nitems, ngrp - 1, rows, CHUNK), jnp.float32),
            dma((nk + 1,)),
            dma((nitems,)),
            dma((4, nk)),
            dma((5, nk)),
            dma((5, nk)),
            dma((5, nk)),
            dma((nk,)),
            dma,
            dma,
            dma((nitems, ngrp - 1)),
            dma((nitems, ngrp - 1)),
        ],
        compiler_params=pltpu.CompilerParams(
            collective_id=0, has_side_effects=True, vmem_limit_bytes=60 * 1024 * 1024
        ),
    )(band, z, zt)


def on_device(nblk, nsamp, dosage, observed, band):
    depth, width = dosage.shape
    weight = observed.astype(jnp.float32)
    values = dosage.astype(jnp.float32)
    cnt, first, second = lax.psum(
        (
            jnp.sum(weight, axis=0),
            jnp.sum(weight * values, axis=0),
            jnp.sum(weight * values * values, axis=0),
        ),
        "samp",
    )
    mean = first / cnt
    spread = second - first * mean
    zed = (weight * (values - mean) * lax.rsqrt(spread + eps * cnt)).astype(jnp.bfloat16)
    turned = zed.T.reshape(nsamp // 2, 2, width // nsamp, depth)
    return linkage_of(zed, turned, band, nblk, nsamp)


def solution(mesh):
    return jax.shard_map(
        functools.partial(on_device, mesh.shape["snp"], mesh.shape["samp"]),
        mesh=mesh,
        in_specs=(P("samp", "snp"), P("samp", "snp"), P()),
        out_specs=P(("snp", "samp"), None),
        check_vma=False,
    )
```

```python
import functools

import jax
import jax.numpy as jnp
from jax import lax
from jax.experimental import pallas as pl
from jax.experimental.pallas import tpu as pltpu
from jax.sharding import PartitionSpec as P

eps = 1e-05
MESH = pl.DeviceIdType.MESH
CHUNK = 256


def offset_of(slot, e):
    return jnp.where(slot == 1, -e, jnp.where(slot == 2, -2 * e, jnp.where(slot == 3, 2 * e, jnp.where(slot == 4, e, 0))))


def linkage_kernel(
    nblk, nsamp, nk, band_ref, dosage_ref, observed_ref, out_ref,
    dosages, marks, stats, right, turned, left_in, acc, part_out, part_in,
    dosage_sem, mark_sem, stat_send, stat_recv, out_sem, z_send, z_recv, fwd_send, fwd_recv, relay_send, left_send, left_recv, part_send, part_recv,
):
    b = lax.axis_index("snp")
    s = lax.axis_index("samp")
    ngrp = nsamp // 2
    c = s % 2
    g = s // 2
    mate = s + 1 - 2 * c
    e = 2 * (b % 2) - 1
    width = nk * CHUNK
    nitems = 5 * nk

    def inside(block):
        return (block >= 0) & (block < nblk)

    def has(slot):
        return inside(b + offset_of(slot, e))

    def item(i):
        j = i - nk
        slot = jnp.where(i < nk, 0, jnp.where(j < 3 * nk, 1 + j % 3, 4))
        return slot, jnp.where(i < nk, i, jnp.where(j < 3 * nk, j // 3, j - 3 * nk))

    def load(k):
        columns = pl.ds(k * CHUNK, CHUNK)
        return (
            pltpu.make_async_copy(dosage_ref.at[:, columns], dosages.at[k], dosage_sem.at[k]),
            pltpu.make_async_copy(observed_ref.at[:, columns], marks.at[k], mark_sem.at[k]),
        )

    for k in range(nk):
        for copy in load(k):
            copy.start()

    barrier = pltpu.get_barrier_semaphore()
    for j in range(1, nsamp):
        pl.semaphore_signal(barrier, inc=1, device_id=(b, (s + j) % nsamp), device_id_type=MESH)
    for by in (-2, -1, 1, 2):
        @pl.when(inside(b + by))
        def _():
            pl.semaphore_signal(barrier, inc=1, device_id=(b + by, s), device_id_type=MESH)

    depth = dosages.shape[1]
    lanes = 128

    for k in range(nk):
        for copy in load(k):
            copy.wait()

        def add_rows(r, sums):
            at = pl.ds(pl.multiple_of(r * lanes, lanes), lanes)
            weight = marks[k, at, :].astype(jnp.float32)
            first = weight * dosages[k, at, :].astype(jnp.float32)
            second = first * dosages[k, at, :].astype(jnp.float32)
            return tuple(
                total + jnp.sum(term.reshape(lanes // 8, 8, CHUNK), axis=0)
                for total, term in zip(sums, (weight, first, second))
            )

        zero = jnp.zeros((8, CHUNK), jnp.float32)
        sums = lax.fori_loop(0, depth // lanes, add_rows, (zero, zero, zero))
        for q in range(3):
            stats[s, q : q + 1, k * CHUNK : (k + 1) * CHUNK] = jnp.sum(sums[q], axis=0, keepdims=True)
    stats[s, 3:8, :] = jnp.zeros((5, width), jnp.float32)

    beside = [jnp.where(inside(b + by), 1, 0) for by in (-2, -1, 1, 2)]
    pl.semaphore_wait(barrier, nsamp - 1 + sum(beside))

    def tell(j):
        return pltpu.make_async_remote_copy(
            stats.at[s], stats.at[s], stat_send.at[j - 1], stat_recv.at[j - 1],
            device_id=(b, (s + j) % nsamp), device_id_type=MESH)

    def hear(j):
        other = (s + nsamp - j) % nsamp
        return pltpu.make_async_remote_copy(
            stats.at[other], stats.at[other], stat_send.at[j - 1], stat_recv.at[j - 1],
            device_id=(b, other), device_id_type=MESH)

    for j in range(1, nsamp):
        tell(j).start()

    mate_left = pltpu.make_async_remote_copy(
        turned.at[1 - c], left_in, left_send, left_recv, device_id=(b, mate), device_id_type=MESH)

    def direct(way, k):
        target = b + (-e, 2 * e, -2 * e)[way - 1]
        return target, pltpu.make_async_remote_copy(
            right.at[0, c, k], right.at[way, c, k], z_send.at[way, k], z_recv.at[way, k],
            device_id=(target, s), device_id_type=MESH)

    def relay(source, target, k):
        return pltpu.make_async_remote_copy(
            right.at[source, c, k], right.at[4, c, k], relay_send.at[k], z_recv.at[4, k],
            device_id=(target, s), device_id_type=MESH)

    def arrival(slot, k):
        return pltpu.make_async_remote_copy(
            right.at[slot, c, k], right.at[slot, c, k], z_send.at[slot, k], z_recv.at[slot, k],
            device_id=(b, mate), device_id_type=MESH)

    def forward(slot, k):
        return pltpu.make_async_remote_copy(
            right.at[slot, c, k], right.at[slot, c, k], fwd_send.at[slot, k], fwd_recv.at[slot, k],
            device_id=(b, mate), device_id_type=MESH)

    def forward_in(slot, k):
        return pltpu.make_async_remote_copy(
            right.at[slot, 1 - c, k], right.at[slot, 1 - c, k], fwd_send.at[slot, k], fwd_recv.at[slot, k],
            device_id=(b, mate), device_id_type=MESH)

    for j in range(1, nsamp):
        hear(j).wait_recv()
    whole = stats[0]
    for other in range(1, nsamp):
        whole = whole + stats[other]

    for k in range(nk):
        part = whole[:, k * CHUNK : (k + 1) * CHUNK]
        cnt, first, second = part[0:1], part[1:2], part[2:3]
        mean = first / cnt
        scale = lax.rsqrt(second - first * mean + eps * cnt)

        def standardize(r, carry):
            at = pl.ds(pl.multiple_of(r * lanes, lanes), lanes)
            weight = marks[k, at, :].astype(jnp.float32)
            values = dosages[k, at, :].astype(jnp.float32)
            right[0, c, k, at, :] = (weight * (values - mean) * scale).astype(jnp.bfloat16)
            return carry

        lax.fori_loop(0, depth // lanes, standardize, 0)
        forward(0, k).start()
        for way in (1, 2, 3):
            target, copy = direct(way, k)

            @pl.when(inside(target))
            def _():
                copy.start()

    rows_each = width // nsamp
    for k in range(nk):
        def turn(r, carry):
            at = pl.ds(pl.multiple_of(r * lanes, lanes), lanes)
            flipped = right[0, c, k, at, :].T
            for t in range(CHUNK // rows_each):
                owner = k * (CHUNK // rows_each) + t
                turned[owner % 2, owner // 2, :, at] = flipped[t * rows_each : (t + 1) * rows_each]
            return carry

        lax.fori_loop(0, depth // lanes, turn, 0)
    mate_left.start()

    def receive(i):
        slot, k = item(i)

        @pl.when((slot > 0) & has(slot))
        def _():
            arrival(slot, k).wait_recv()
            forward(slot, k).start()

            @pl.when((slot == 2) & (k % 2 == 0))
            def _():
                relay(2, b - e, k).start()

            @pl.when((slot == 1) & (k % 2 == 1) & has(2))
            def _():
                relay(1, b - 2 * e, k).start()

    def partial(i, j):
        return pltpu.make_async_remote_copy(
            part_out.at[i, j - 1], part_in.at[i, j - 1], part_send.at[i, j - 1], part_recv.at[i, j - 1],
            device_id=(b, 2 * ((g + j) % ngrp) + c), device_id_type=MESH)

    def multiply(i):
        slot, k = item(i)

        @pl.when(has(slot))
        def _():
            forward_in(slot, k).wait_recv()

            def rows(group):
                return jnp.dot(
                    turned[c, group], right[slot, c, k], preferred_element_type=jnp.float32
                ) + jnp.dot(left_in[group], right[slot, 1 - c, k], preferred_element_type=jnp.float32)

            for j in range(1, ngrp):
                part_out[i, j - 1] = rows((g + j) % ngrp)
                partial(i, j).start()
            acc[i] = rows(g)

    mate_left.wait_recv()

    def step(i, carry):
        @pl.when(i + 1 < nitems)
        def _():
            receive(i + 1)
        multiply(i)
        return carry

    lax.fori_loop(0, nitems, step, 0)

    def store(i):
        slot, k = item(i)
        column = (offset_of(slot, e) + 2) * width + k * CHUNK
        return pltpu.make_async_copy(acc.at[i], out_ref.at[:, pl.ds(pl.multiple_of(column, CHUNK), CHUNK)], out_sem.at[i])

    def finish(i, carry):
        slot, k = item(i)

        @pl.when(has(slot))
        def _():
            total = acc[i]
            for j in range(1, ngrp):
                partial(i, j).wait_recv()
                total = total + part_in[i, j - 1]
            offset = offset_of(slot, e)
            kept = jnp.abs(offset) <= jnp.minimum(band_ref[b], band_ref[b + offset])
            acc[i] = total * jnp.where(kept, 1.0, 0.0).astype(jnp.float32)

        @pl.when(jnp.logical_not(has(slot)))
        def _():
            acc[i] = jnp.zeros(acc.shape[1:], acc.dtype)
        store(i).start()
        return carry

    lax.fori_loop(0, nitems, finish, 0)

    def drain(i, carry):
        slot, k = item(i)
        store(i).wait()

        @pl.when(has(slot))
        def _():
            forward(slot, k).wait_send()
            for j in range(1, ngrp):
                partial(i, j).wait_send()
        return carry

    lax.fori_loop(0, nitems, drain, 0)
    mate_left.wait_send()
    for j in range(1, nsamp):
        tell(j).wait_send()
    for k in range(nk):
        for way in (1, 2, 3):
            target, copy = direct(way, k)

            @pl.when(inside(target))
            def _():
                copy.wait_send()

        @pl.when(has(2))
        def _():
            relay(2, b - e, k).wait_send()


def on_device(nblk, nsamp, dosage, observed, band):
    depth, width = dosage.shape
    nk = width // CHUNK
    ngrp = nsamp // 2
    rows = width // nsamp
    nitems = 5 * nk
    dma = pltpu.SemaphoreType.DMA
    return pl.pallas_call(
        functools.partial(linkage_kernel, nblk, nsamp, nk),
        out_shape=jax.ShapeDtypeStruct((rows, 5 * width), jnp.float32),
        in_specs=[
            pl.BlockSpec(memory_space=pltpu.SMEM),
            pl.BlockSpec(memory_space=pl.ANY),
            pl.BlockSpec(memory_space=pl.ANY),
        ],
        out_specs=pl.BlockSpec(memory_space=pl.ANY),
        scratch_shapes=[
            pltpu.VMEM((nk, depth, CHUNK), jnp.bfloat16),
            pltpu.VMEM((nk, depth, CHUNK), jnp.int32),
            pltpu.VMEM((nsamp, 8, width), jnp.float32),
            pltpu.VMEM((5, 2, nk, depth, CHUNK), jnp.bfloat16),
            pltpu.VMEM((2, ngrp, rows, depth), jnp.bfloat16),
            pltpu.VMEM((ngrp, rows, depth), jnp.bfloat16),
            pltpu.VMEM((nitems, rows, CHUNK), jnp.float32),
            pltpu.VMEM((nitems, ngrp - 1, rows, CHUNK), jnp.float32),
            pltpu.VMEM((nitems, ngrp - 1, rows, CHUNK), jnp.float32),
            dma((nk,)),
            dma((nk,)),
            dma((nsamp - 1,)),
            dma((nsamp - 1,)),
            dma((nitems,)),
            dma((4, nk)),
            dma((5, nk)),
            dma((5, nk)),
            dma((5, nk)),
            dma((nk,)),
            dma,
            dma,
            dma((nitems, ngrp - 1)),
            dma((nitems, ngrp - 1)),
        ],
        compiler_params=pltpu.CompilerParams(
            collective_id=0, has_side_effects=True, vmem_limit_bytes=60 * 1024 * 1024
        ),
    )(band, dosage, observed)


def solution(mesh):
    return jax.shard_map(
        functools.partial(on_device, mesh.shape["snp"], mesh.shape["samp"]),
        mesh=mesh,
        in_specs=(P("samp", "snp"), P("samp", "snp"), P()),
        out_specs=P(("snp", "samp"), None),
        check_vma=False,
    )
```

```python
import functools

import jax
import jax.numpy as jnp
from jax import lax
from jax.experimental import pallas as pl
from jax.experimental.pallas import tpu as pltpu
from jax.sharding import PartitionSpec as P

eps = 1e-05
MESH = pl.DeviceIdType.MESH
CHUNK = 256


def offset_of(slot, e):
    return jnp.where(slot == 1, -e, jnp.where(slot == 2, -2 * e, jnp.where(slot == 3, 2 * e, jnp.where(slot == 4, e, 0))))


def linkage_kernel(
    nblk, nsamp, nk, band_ref, dosage_ref, observed_ref, out_ref,
    dosages, marks, stats, right, turned, left_in, acc, part_out, part_in,
    dosage_sem, mark_sem, stat_send, stat_recv, out_sem, z_send, z_recv, fwd_send, fwd_recv, relay_send, left_send, left_recv, part_send, part_recv,
):
    b = lax.axis_index("snp")
    s = lax.axis_index("samp")
    ngrp = nsamp // 2
    c = s % 2
    g = s // 2
    mate = s + 1 - 2 * c
    e = 2 * (b % 2) - 1
    width = nk * CHUNK
    nitems = 5 * nk

    def inside(block):
        return (block >= 0) & (block < nblk)

    def has(slot):
        return inside(b + offset_of(slot, e))

    def item(i):
        j = i - nk
        slot = jnp.where(i < nk, 0, jnp.where(j < 3 * nk, 1 + j % 3, 4))
        return slot, jnp.where(i < nk, i, jnp.where(j < 3 * nk, j // 3, j - 3 * nk))

    def load(k):
        columns = pl.ds(k * CHUNK, CHUNK)
        return (
            pltpu.make_async_copy(dosage_ref.at[:, columns], dosages.at[k], dosage_sem.at[k]),
            pltpu.make_async_copy(observed_ref.at[:, columns], marks.at[k], mark_sem.at[k]),
        )

    for k in range(nk):
        for copy in load(k):
            copy.start()

    barrier = pltpu.get_barrier_semaphore()
    for j in range(1, nsamp):
        pl.semaphore_signal(barrier, inc=1, device_id=(b, (s + j) % nsamp), device_id_type=MESH)
    for by in (-2, -1, 1, 2):
        @pl.when(inside(b + by))
        def _():
            pl.semaphore_signal(barrier, inc=1, device_id=(b + by, s), device_id_type=MESH)

    depth = dosages.shape[1]
    lanes = 128

    for k in range(nk):
        for copy in load(k):
            copy.wait()

        def add_rows(r, sums):
            at = pl.ds(pl.multiple_of(r * lanes, lanes), lanes)
            weight = marks[k, at, :].astype(jnp.float32)
            first = weight * dosages[k, at, :].astype(jnp.float32)
            second = first * dosages[k, at, :].astype(jnp.float32)
            return tuple(
                total + jnp.sum(term.reshape(lanes // 8, 8, CHUNK), axis=0)
                for total, term in zip(sums, (weight, first, second))
            )

        zero = jnp.zeros((8, CHUNK), jnp.float32)
        sums = lax.fori_loop(0, depth // lanes, add_rows, (zero, zero, zero))
        for q in range(3):
            stats[s, q : q + 1, k * CHUNK : (k + 1) * CHUNK] = jnp.sum(sums[q], axis=0, keepdims=True)
    stats[s, 3:8, :] = jnp.zeros((5, width), jnp.float32)

    beside = [jnp.where(inside(b + by), 1, 0) for by in (-2, -1, 1, 2)]
    pl.semaphore_wait(barrier, nsamp - 1 + sum(beside))

    def tell(j):
        return pltpu.make_async_remote_copy(
            stats.at[s], stats.at[s], stat_send.at[j - 1], stat_recv.at[j - 1],
            device_id=(b, (s + j) % nsamp), device_id_type=MESH)

    def hear(j):
        other = (s + nsamp - j) % nsamp
        return pltpu.make_async_remote_copy(
            stats.at[other], stats.at[other], stat_send.at[j - 1], stat_recv.at[j - 1],
            device_id=(b, other), device_id_type=MESH)

    for j in range(1, nsamp):
        tell(j).start()

    def mate_left(group):
        return pltpu.make_async_remote_copy(
            turned.at[1 - c, group], left_in.at[group], left_send.at[group], left_recv.at[group],
            device_id=(b, mate), device_id_type=MESH)

    def direct(way, k):
        target = b + (-e, 2 * e, -2 * e)[way - 1]
        return target, pltpu.make_async_remote_copy(
            right.at[0, c, k], right.at[way, c, k], z_send.at[way, k], z_recv.at[way, k],
            device_id=(target, s), device_id_type=MESH)

    def relay(source, target, k):
        return pltpu.make_async_remote_copy(
            right.at[source, c, k], right.at[4, c, k], relay_send.at[k], z_recv.at[4, k],
            device_id=(target, s), device_id_type=MESH)

    def arrival(slot, k):
        return pltpu.make_async_remote_copy(
            right.at[slot, c, k], right.at[slot, c, k], z_send.at[slot, k], z_recv.at[slot, k],
            device_id=(b, mate), device_id_type=MESH)

    def forward(slot, k):
        return pltpu.make_async_remote_copy(
            right.at[slot, c, k], right.at[slot, c, k], fwd_send.at[slot, k], fwd_recv.at[slot, k],
            device_id=(b, mate), device_id_type=MESH)

    def forward_in(slot, k):
        return pltpu.make_async_remote_copy(
            right.at[slot, 1 - c, k], right.at[slot, 1 - c, k], fwd_send.at[slot, k], fwd_recv.at[slot, k],
            device_id=(b, mate), device_id_type=MESH)

    for j in range(1, nsamp):
        hear(j).wait_recv()
    whole = stats[0]
    for other in range(1, nsamp):
        whole = whole + stats[other]

    rows_each = width // nsamp
    each = CHUNK // rows_each
    for k in range(nk):
        part = whole[:, k * CHUNK : (k + 1) * CHUNK]
        cnt, first, second = part[0:1], part[1:2], part[2:3]
        mean = first / cnt
        scale = lax.rsqrt(second - first * mean + eps * cnt)

        def standardize(r, carry):
            at = pl.ds(pl.multiple_of(r * lanes, lanes), lanes)
            weight = marks[k, at, :].astype(jnp.float32)
            values = dosages[k, at, :].astype(jnp.float32)
            zed = (weight * (values - mean) * scale).astype(jnp.bfloat16)
            right[0, c, k, at, :] = zed
            flipped = zed.T
            for t in range(each):
                owner = k * each + t
                turned[owner % 2, owner // 2, :, at] = flipped[t * rows_each : (t + 1) * rows_each]
            return carry

        lax.fori_loop(0, depth // lanes, standardize, 0)
        if k == 0:
            forward(0, k).start()
        for group in range(k * each // 2, (k + 1) * each // 2):
            mate_left(group).start()
        for way in (1, 2, 3):
            target, copy = direct(way, k)

            @pl.when(inside(target))
            def _():
                copy.start()

    for k in range(1, nk):
        forward(0, k).start()

    def receive(i):
        slot, k = item(i)

        @pl.when((slot > 0) & has(slot))
        def _():
            arrival(slot, k).wait_recv()
            forward(slot, k).start()

            @pl.when((slot == 2) & (k % 2 == 0))
            def _():
                relay(2, b - e, k).start()

            @pl.when((slot == 1) & (k % 2 == 1) & has(2))
            def _():
                relay(1, b - 2 * e, k).start()

    def partial(i, j):
        return pltpu.make_async_remote_copy(
            part_out.at[i, j - 1], part_in.at[i, j - 1], part_send.at[i, j - 1], part_recv.at[i, j - 1],
            device_id=(b, 2 * ((g + j) % ngrp) + c), device_id_type=MESH)

    def multiply(i):
        slot, k = item(i)

        @pl.when(has(slot))
        def _():
            forward_in(slot, k).wait_recv()

            def rows(group):
                return jnp.dot(
                    turned[c, group], right[slot, c, k], preferred_element_type=jnp.float32
                ) + jnp.dot(left_in[group], right[slot, 1 - c, k], preferred_element_type=jnp.float32)

            for j in range(1, ngrp):
                part_out[i, j - 1] = rows((g + j) % ngrp)
                partial(i, j).start()
            acc[i] = rows(g)

    for group in range(ngrp):
        mate_left(group).wait_recv()

    def step(i, carry):
        @pl.when(i + 1 < nitems)
        def _():
            receive(i + 1)
        multiply(i)
        return carry

    lax.fori_loop(0, nitems, step, 0)

    def store(i):
        slot, k = item(i)
        column = (offset_of(slot, e) + 2) * width + k * CHUNK
        return pltpu.make_async_copy(acc.at[i], out_ref.at[:, pl.ds(pl.multiple_of(column, CHUNK), CHUNK)], out_sem.at[i])

    def finish(i, carry):
        slot, k = item(i)

        @pl.when(has(slot))
        def _():
            total = acc[i]
            for j in range(1, ngrp):
                partial(i, j).wait_recv()
                total = total + part_in[i, j - 1]
            offset = offset_of(slot, e)
            kept = jnp.abs(offset) <= jnp.minimum(band_ref[b], band_ref[b + offset])
            acc[i] = total * jnp.where(kept, 1.0, 0.0).astype(jnp.float32)

        @pl.when(jnp.logical_not(has(slot)))
        def _():
            acc[i] = jnp.zeros(acc.shape[1:], acc.dtype)
        store(i).start()
        return carry

    lax.fori_loop(0, nitems, finish, 0)

    def drain(i, carry):
        slot, k = item(i)
        store(i).wait()

        @pl.when(has(slot))
        def _():
            forward(slot, k).wait_send()
            for j in range(1, ngrp):
                partial(i, j).wait_send()
        return carry

    lax.fori_loop(0, nitems, drain, 0)
    for group in range(ngrp):
        mate_left(group).wait_send()
    for j in range(1, nsamp):
        tell(j).wait_send()
    for k in range(nk):
        for way in (1, 2, 3):
            target, copy = direct(way, k)

            @pl.when(inside(target))
            def _():
                copy.wait_send()

        @pl.when(has(2))
        def _():
            relay(2, b - e, k).wait_send()


def on_device(nblk, nsamp, dosage, observed, band):
    depth, width = dosage.shape
    nk = width // CHUNK
    ngrp = nsamp // 2
    rows = width // nsamp
    nitems = 5 * nk
    dma = pltpu.SemaphoreType.DMA
    return pl.pallas_call(
        functools.partial(linkage_kernel, nblk, nsamp, nk),
        out_shape=jax.ShapeDtypeStruct((rows, 5 * width), jnp.float32),
        in_specs=[
            pl.BlockSpec(memory_space=pltpu.SMEM),
            pl.BlockSpec(memory_space=pl.ANY),
            pl.BlockSpec(memory_space=pl.ANY),
        ],
        out_specs=pl.BlockSpec(memory_space=pl.ANY),
        scratch_shapes=[
            pltpu.VMEM((nk, depth, CHUNK), jnp.bfloat16),
            pltpu.VMEM((nk, depth, CHUNK), jnp.int32),
            pltpu.VMEM((nsamp, 8, width), jnp.float32),
            pltpu.VMEM((5, 2, nk, depth, CHUNK), jnp.bfloat16),
            pltpu.VMEM((2, ngrp, rows, depth), jnp.bfloat16),
            pltpu.VMEM((ngrp, rows, depth), jnp.bfloat16),
            pltpu.VMEM((nitems, rows, CHUNK), jnp.float32),
            pltpu.VMEM((nitems, ngrp - 1, rows, CHUNK), jnp.float32),
            pltpu.VMEM((nitems, ngrp - 1, rows, CHUNK), jnp.float32),
            dma((nk,)),
            dma((nk,)),
            dma((nsamp - 1,)),
            dma((nsamp - 1,)),
            dma((nitems,)),
            dma((4, nk)),
            dma((5, nk)),
            dma((5, nk)),
            dma((5, nk)),
            dma((nk,)),
            dma((ngrp,)),
            dma((ngrp,)),
            dma((nitems, ngrp - 1)),
            dma((nitems, ngrp - 1)),
        ],
        compiler_params=pltpu.CompilerParams(
            collective_id=0, has_side_effects=True, vmem_limit_bytes=60 * 1024 * 1024
        ),
    )(band, dosage, observed)


def solution(mesh):
    return jax.shard_map(
        functools.partial(on_device, mesh.shape["snp"], mesh.shape["samp"]),
        mesh=mesh,
        in_specs=(P("samp", "snp"), P("samp", "snp"), P()),
        out_specs=P(("snp", "samp"), None),
        check_vma=False,
    )
```

```python
import functools

import jax
import jax.numpy as jnp
from jax import lax
from jax.experimental import pallas as pl
from jax.experimental.pallas import tpu as pltpu
from jax.sharding import PartitionSpec as P

eps = 1e-05
MESH = pl.DeviceIdType.MESH
CHUNK = 256


def offset_of(slot, e):
    return jnp.where(slot == 1, -e, jnp.where(slot == 2, -2 * e, jnp.where(slot == 3, 2 * e, jnp.where(slot == 4, e, 0))))


def linkage_kernel(
    nblk, nsamp, nk, band_ref, dosage_ref, observed_ref, out_ref,
    dosages, marks, stats, right, turned, left_in, acc, part_out, part_in,
    dosage_sem, mark_sem, stat_send, stat_recv, out_sem, z_send, z_recv, fwd_send, fwd_recv, relay_send, left_send, left_recv, part_send, part_recv,
):
    b = lax.axis_index("snp")
    s = lax.axis_index("samp")
    ngrp = nsamp // 2
    c = s % 2
    g = s // 2
    mate = s + 1 - 2 * c
    e = 2 * (b % 2) - 1
    width = nk * CHUNK
    nitems = 5 * nk

    def inside(block):
        return (block >= 0) & (block < nblk)

    def has(slot):
        return inside(b + offset_of(slot, e))

    def item(i):
        j = i - nk
        slot = jnp.where(i < nk, 0, jnp.where(j < 3 * nk, 1 + j % 3, 4))
        return slot, jnp.where(i < nk, i, jnp.where(j < 3 * nk, j // 3, j - 3 * nk))

    def load(k):
        columns = pl.ds(k * CHUNK, CHUNK)
        return (
            pltpu.make_async_copy(dosage_ref.at[:, columns], dosages.at[k], dosage_sem.at[k]),
            pltpu.make_async_copy(observed_ref.at[:, columns], marks.at[k], mark_sem.at[k]),
        )

    for k in range(nk):
        for copy in load(k):
            copy.start()

    barrier = pltpu.get_barrier_semaphore()
    for j in range(1, nsamp):
        pl.semaphore_signal(barrier, inc=1, device_id=(b, (s + j) % nsamp), device_id_type=MESH)
    for by in (-2, -1, 1, 2):
        @pl.when(inside(b + by))
        def _():
            pl.semaphore_signal(barrier, inc=1, device_id=(b + by, s), device_id_type=MESH)

    depth = dosages.shape[1]
    lanes = 128

    def tell(j, k):
        return pltpu.make_async_remote_copy(
            stats.at[s, k], stats.at[s, k], stat_send.at[j - 1, k], stat_recv.at[j - 1, k],
            device_id=(b, (s + j) % nsamp), device_id_type=MESH)

    def hear(j, k):
        other = (s + nsamp - j) % nsamp
        return pltpu.make_async_remote_copy(
            stats.at[other, k], stats.at[other, k], stat_send.at[j - 1, k], stat_recv.at[j - 1, k],
            device_id=(b, other), device_id_type=MESH)

    for k in range(nk):
        for copy in load(k):
            copy.wait()

        def add_rows(r, sums):
            at = pl.ds(pl.multiple_of(r * lanes, lanes), lanes)
            weight = marks[k, at, :].astype(jnp.float32)
            first = weight * dosages[k, at, :].astype(jnp.float32)
            second = first * dosages[k, at, :].astype(jnp.float32)
            return tuple(
                total + jnp.sum(term.reshape(lanes // 8, 8, CHUNK), axis=0)
                for total, term in zip(sums, (weight, first, second))
            )

        zero = jnp.zeros((8, CHUNK), jnp.float32)
        sums = lax.fori_loop(0, depth // lanes, add_rows, (zero, zero, zero))
        for q in range(3):
            stats[s, k, q : q + 1, :] = jnp.sum(sums[q], axis=0, keepdims=True)
        stats[s, k, 3:8, :] = jnp.zeros((5, CHUNK), jnp.float32)
        if k == 0:
            beside = [jnp.where(inside(b + by), 1, 0) for by in (-2, -1, 1, 2)]
            pl.semaphore_wait(barrier, nsamp - 1 + sum(beside))
        for j in range(1, nsamp):
            tell(j, k).start()

    def mate_left(group):
        return pltpu.make_async_remote_copy(
            turned.at[1 - c, group], left_in.at[group], left_send.at[group], left_recv.at[group],
            device_id=(b, mate), device_id_type=MESH)

    def direct(way, k):
        target = b + (-e, 2 * e, -2 * e)[way - 1]
        return target, pltpu.make_async_remote_copy(
            right.at[0, c, k], right.at[way, c, k], z_send.at[way, k], z_recv.at[way, k],
            device_id=(target, s), device_id_type=MESH)

    def relay(source, target, k):
        return pltpu.make_async_remote_copy(
            right.at[source, c, k], right.at[4, c, k], relay_send.at[k], z_recv.at[4, k],
            device_id=(target, s), device_id_type=MESH)

    def arrival(slot, k):
        return pltpu.make_async_remote_copy(
            right.at[slot, c, k], right.at[slot, c, k], z_send.at[slot, k], z_recv.at[slot, k],
            device_id=(b, mate), device_id_type=MESH)

    def forward(slot, k):
        return pltpu.make_async_remote_copy(
            right.at[slot, c, k], right.at[slot, c, k], fwd_send.at[slot, k], fwd_recv.at[slot, k],
            device_id=(b, mate), device_id_type=MESH)

    def forward_in(slot, k):
        return pltpu.make_async_remote_copy(
            right.at[slot, 1 - c, k], right.at[slot, 1 - c, k], fwd_send.at[slot, k], fwd_recv.at[slot, k],
            device_id=(b, mate), device_id_type=MESH)

    rows_each = width // nsamp
    each = CHUNK // rows_each
    for k in range(nk):
        for j in range(1, nsamp):
            hear(j, k).wait_recv()
        part = stats[0, k]
        for other in range(1, nsamp):
            part = part + stats[other, k]
        cnt, first, second = part[0:1], part[1:2], part[2:3]
        mean = first / cnt
        scale = lax.rsqrt(second - first * mean + eps * cnt)

        def standardize(r, carry):
            at = pl.ds(pl.multiple_of(r * lanes, lanes), lanes)
            weight = marks[k, at, :].astype(jnp.float32)
            values = dosages[k, at, :].astype(jnp.float32)
            zed = (weight * (values - mean) * scale).astype(jnp.bfloat16)
            right[0, c, k, at, :] = zed
            flipped = zed.T
            for t in range(each):
                owner = k * each + t
                turned[owner % 2, owner // 2, :, at] = flipped[t * rows_each : (t + 1) * rows_each]
            return carry

        lax.fori_loop(0, depth // lanes, standardize, 0)
        if k == 0:
            forward(0, k).start()
        for group in range(k * each // 2, (k + 1) * each // 2):
            mate_left(group).start()
        for way in (1, 2, 3):
            target, copy = direct(way, k)

            @pl.when(inside(target))
            def _():
                copy.start()

    for k in range(1, nk):
        forward(0, k).start()

    def receive(i):
        slot, k = item(i)

        @pl.when((slot > 0) & has(slot))
        def _():
            arrival(slot, k).wait_recv()
            forward(slot, k).start()

            @pl.when((slot == 2) & (k % 2 == 0))
            def _():
                relay(2, b - e, k).start()

            @pl.when((slot == 1) & (k % 2 == 1) & has(2))
            def _():
                relay(1, b - 2 * e, k).start()

    def partial(i, j):
        return pltpu.make_async_remote_copy(
            part_out.at[i, j - 1], part_in.at[i, j - 1], part_send.at[i, j - 1], part_recv.at[i, j - 1],
            device_id=(b, 2 * ((g + j) % ngrp) + c), device_id_type=MESH)

    def multiply(i):
        slot, k = item(i)

        @pl.when(has(slot))
        def _():
            forward_in(slot, k).wait_recv()

            def rows(group):
                return jnp.dot(
                    turned[c, group], right[slot, c, k], preferred_element_type=jnp.float32
                ) + jnp.dot(left_in[group], right[slot, 1 - c, k], preferred_element_type=jnp.float32)

            for j in range(1, ngrp):
                part_out[i, j - 1] = rows((g + j) % ngrp)
                partial(i, j).start()
            acc[i] = rows(g)

    for group in range(ngrp):
        mate_left(group).wait_recv()

    def step(i, carry):
        @pl.when(i + 1 < nitems)
        def _():
            receive(i + 1)
        multiply(i)
        return carry

    lax.fori_loop(0, nitems, step, 0)

    def store(i):
        slot, k = item(i)
        column = (offset_of(slot, e) + 2) * width + k * CHUNK
        return pltpu.make_async_copy(acc.at[i], out_ref.at[:, pl.ds(pl.multiple_of(column, CHUNK), CHUNK)], out_sem.at[i])

    def finish(i, carry):
        slot, k = item(i)

        @pl.when(has(slot))
        def _():
            total = acc[i]
            for j in range(1, ngrp):
                partial(i, j).wait_recv()
                total = total + part_in[i, j - 1]
            offset = offset_of(slot, e)
            kept = jnp.abs(offset) <= jnp.minimum(band_ref[b], band_ref[b + offset])
            acc[i] = total * jnp.where(kept, 1.0, 0.0).astype(jnp.float32)

        @pl.when(jnp.logical_not(has(slot)))
        def _():
            acc[i] = jnp.zeros(acc.shape[1:], acc.dtype)
        store(i).start()
        return carry

    lax.fori_loop(0, nitems, finish, 0)

    def drain(i, carry):
        slot, k = item(i)
        store(i).wait()

        @pl.when(has(slot))
        def _():
            forward(slot, k).wait_send()
            for j in range(1, ngrp):
                partial(i, j).wait_send()
        return carry

    lax.fori_loop(0, nitems, drain, 0)
    for group in range(ngrp):
        mate_left(group).wait_send()
    for j in range(1, nsamp):
        for k in range(nk):
            tell(j, k).wait_send()
    for k in range(nk):
        for way in (1, 2, 3):
            target, copy = direct(way, k)

            @pl.when(inside(target))
            def _():
                copy.wait_send()

        @pl.when(has(2))
        def _():
            relay(2, b - e, k).wait_send()


def hand_on(in_ref, out_ref):
    out_ref[...] = in_ref[...]


def on_device(nblk, nsamp, dosage, observed, band):
    depth, width = dosage.shape
    nk = width // CHUNK
    ngrp = nsamp // 2
    rows = width // nsamp
    nitems = 5 * nk
    dma = pltpu.SemaphoreType.DMA
    linkage = pl.pallas_call(
        functools.partial(linkage_kernel, nblk, nsamp, nk),
        out_shape=jax.ShapeDtypeStruct((rows, 5 * width), jnp.float32),
        in_specs=[
            pl.BlockSpec(memory_space=pltpu.SMEM),
            pl.BlockSpec(memory_space=pl.ANY),
            pl.BlockSpec(memory_space=pl.ANY),
        ],
        out_specs=pl.BlockSpec(memory_space=pl.ANY),
        scratch_shapes=[
            pltpu.VMEM((nk, depth, CHUNK), jnp.bfloat16),
            pltpu.VMEM((nk, depth, CHUNK), jnp.int32),
            pltpu.VMEM((nsamp, nk, 8, CHUNK), jnp.float32),
            pltpu.VMEM((5, 2, nk, depth, CHUNK), jnp.bfloat16),
            pltpu.VMEM((2, ngrp, rows, depth), jnp.bfloat16),
            pltpu.VMEM((ngrp, rows, depth), jnp.bfloat16),
            pltpu.VMEM((nitems, rows, CHUNK), jnp.float32),
            pltpu.VMEM((nitems, ngrp - 1, rows, CHUNK), jnp.float32),
            pltpu.VMEM((nitems, ngrp - 1, rows, CHUNK), jnp.float32),
            dma((nk,)),
            dma((nk,)),
            dma((nsamp - 1, nk)),
            dma((nsamp - 1, nk)),
            dma((nitems,)),
            dma((4, nk)),
            dma((5, nk)),
            dma((5, nk)),
            dma((5, nk)),
            dma((nk,)),
            dma((ngrp,)),
            dma((ngrp,)),
            dma((nitems, ngrp - 1)),
            dma((nitems, ngrp - 1)),
        ],
        compiler_params=pltpu.CompilerParams(
            collective_id=0, has_side_effects=True, vmem_limit_bytes=60 * 1024 * 1024
        ),
    )(band, dosage, observed)
    block = pl.BlockSpec((rows // 8, 5 * width), lambda i: (i, 0))
    return pl.pallas_call(
        hand_on, out_shape=jax.ShapeDtypeStruct(linkage.shape, linkage.dtype), grid=(8,), in_specs=[block], out_specs=block
    )(linkage)


def solution(mesh):
    return jax.shard_map(
        functools.partial(on_device, mesh.shape["snp"], mesh.shape["samp"]),
        mesh=mesh,
        in_specs=(P("samp", "snp"), P("samp", "snp"), P()),
        out_specs=P(("snp", "samp"), None),
        check_vma=False,
    )
```

```python
import functools

import jax
import jax.numpy as jnp
from jax import lax
from jax.experimental import pallas as pl
from jax.experimental.pallas import tpu as pltpu
from jax.sharding import PartitionSpec as P

eps = 1e-05
MESH = pl.DeviceIdType.MESH
CHUNK = 256


def offset_of(slot, e):
    return jnp.where(slot == 1, -e, jnp.where(slot == 2, -2 * e, jnp.where(slot == 3, 2 * e, jnp.where(slot == 4, e, 0))))


def linkage_kernel(
    nblk, nsamp, nk, band_ref, dosage_ref, observed_ref, out_ref,
    dosages, marks, stats, right, turned, left_in, acc, part_out, part_in,
    dosage_sem, mark_sem, stat_send, stat_recv, out_sem, z_send, z_recv, fwd_send, fwd_recv, relay_send, left_send, left_recv, part_send, part_recv,
):
    b = lax.axis_index("snp")
    s = lax.axis_index("samp")
    ngrp = nsamp // 2
    c = s % 2
    g = s // 2
    mate = s + 1 - 2 * c
    e = 2 * (b % 2) - 1
    width = nk * CHUNK
    nitems = 5 * nk

    def inside(block):
        return (block >= 0) & (block < nblk)

    def has(slot):
        return inside(b + offset_of(slot, e))

    def item(i):
        j = i - nk
        slot = jnp.where(i < nk, 0, jnp.where(j < 3 * nk, 1 + j % 3, 4))
        return slot, jnp.where(i < nk, i, jnp.where(j < 3 * nk, j // 3, j - 3 * nk))

    def load(k):
        columns = pl.ds(k * CHUNK, CHUNK)
        return (
            pltpu.make_async_copy(dosage_ref.at[:, columns], dosages.at[k], dosage_sem.at[k]),
            pltpu.make_async_copy(observed_ref.at[:, columns], marks.at[k], mark_sem.at[k]),
        )

    for k in range(nk):
        for copy in load(k):
            copy.start()

    barrier = pltpu.get_barrier_semaphore()
    for j in range(1, nsamp):
        pl.semaphore_signal(barrier, inc=1, device_id=(b, (s + j) % nsamp), device_id_type=MESH)
    for by in (-2, -1, 1, 2):
        @pl.when(inside(b + by))
        def _():
            pl.semaphore_signal(barrier, inc=1, device_id=(b + by, s), device_id_type=MESH)

    depth = dosages.shape[1]
    lanes = 128

    def tell(j, k):
        return pltpu.make_async_remote_copy(
            stats.at[s, k], stats.at[s, k], stat_send.at[j - 1, k], stat_recv.at[j - 1, k],
            device_id=(b, (s + j) % nsamp), device_id_type=MESH)

    def hear(j, k):
        other = (s + nsamp - j) % nsamp
        return pltpu.make_async_remote_copy(
            stats.at[other, k], stats.at[other, k], stat_send.at[j - 1, k], stat_recv.at[j - 1, k],
            device_id=(b, other), device_id_type=MESH)

    for k in range(nk):
        for copy in load(k):
            copy.wait()

        def add_rows(r, sums):
            at = pl.ds(pl.multiple_of(r * lanes, lanes), lanes)
            weight = marks[k, at, :].astype(jnp.float32)
            first = weight * dosages[k, at, :].astype(jnp.float32)
            second = first * dosages[k, at, :].astype(jnp.float32)
            return tuple(
                total + jnp.sum(term.reshape(lanes // 8, 8, CHUNK), axis=0)
                for total, term in zip(sums, (weight, first, second))
            )

        zero = jnp.zeros((8, CHUNK), jnp.float32)
        sums = lax.fori_loop(0, depth // lanes, add_rows, (zero, zero, zero))
        for q in range(3):
            stats[s, k, q : q + 1, :] = jnp.sum(sums[q], axis=0, keepdims=True)
        stats[s, k, 3:8, :] = jnp.zeros((5, CHUNK), jnp.float32)
        if k == 0:
            beside = [jnp.where(inside(b + by), 1, 0) for by in (-2, -1, 1, 2)]
            pl.semaphore_wait(barrier, nsamp - 1 + sum(beside))
        for j in range(1, nsamp):
            tell(j, k).start()

    def mate_left(group):
        return pltpu.make_async_remote_copy(
            turned.at[1 - c, group], left_in.at[group], left_send.at[group], left_recv.at[group],
            device_id=(b, mate), device_id_type=MESH)

    def direct(way, k):
        target = b + (-e, 2 * e, -2 * e)[way - 1]
        return target, pltpu.make_async_remote_copy(
            right.at[0, c, k], right.at[way, c, k], z_send.at[way, k], z_recv.at[way, k],
            device_id=(target, s), device_id_type=MESH)

    def relay(source, target, k):
        return pltpu.make_async_remote_copy(
            right.at[source, c, k], right.at[4, c, k], relay_send.at[k], z_recv.at[4, k],
            device_id=(target, s), device_id_type=MESH)

    def arrival(slot, k):
        return pltpu.make_async_remote_copy(
            right.at[slot, c, k], right.at[slot, c, k], z_send.at[slot, k], z_recv.at[slot, k],
            device_id=(b, mate), device_id_type=MESH)

    def forward(slot, k):
        return pltpu.make_async_remote_copy(
            right.at[slot, c, k], right.at[slot, c, k], fwd_send.at[slot, k], fwd_recv.at[slot, k],
            device_id=(b, mate), device_id_type=MESH)

    def forward_in(slot, k):
        return pltpu.make_async_remote_copy(
            right.at[slot, 1 - c, k], right.at[slot, 1 - c, k], fwd_send.at[slot, k], fwd_recv.at[slot, k],
            device_id=(b, mate), device_id_type=MESH)

    rows_each = width // nsamp
    each = CHUNK // rows_each
    for k in range(nk):
        for j in range(1, nsamp):
            hear(j, k).wait_recv()
        part = stats[0, k]
        for other in range(1, nsamp):
            part = part + stats[other, k]
        cnt, first, second = part[0:1], part[1:2], part[2:3]
        mean = first / cnt
        scale = lax.rsqrt(second - first * mean + eps * cnt)

        def standardize(r, carry):
            at = pl.ds(pl.multiple_of(r * lanes, lanes), lanes)
            weight = marks[k, at, :].astype(jnp.float32)
            values = dosages[k, at, :].astype(jnp.float32)
            zed = (weight * (values - mean) * scale).astype(jnp.bfloat16)
            right[0, c, k, at, :] = zed
            flipped = zed.T
            for t in range(each):
                owner = k * each + t
                turned[owner % 2, owner // 2, :, at] = flipped[t * rows_each : (t + 1) * rows_each]
            return carry

        lax.fori_loop(0, depth // lanes, standardize, 0)
        if k == 0:
            forward(0, k).start()
        for group in range(k * each // 2, (k + 1) * each // 2):
            mate_left(group).start()
        for way in (1, 2, 3):
            target, copy = direct(way, k)

            @pl.when(inside(target))
            def _():
                copy.start()

    for k in range(1, nk):
        forward(0, k).start()

    def receive(i):
        slot, k = item(i)

        @pl.when((slot > 0) & has(slot))
        def _():
            arrival(slot, k).wait_recv()
            forward(slot, k).start()

            @pl.when((slot == 2) & (k % 2 == 0))
            def _():
                relay(2, b - e, k).start()

            @pl.when((slot == 1) & (k % 2 == 1) & has(2))
            def _():
                relay(1, b - 2 * e, k).start()

    def partial(i, j):
        return pltpu.make_async_remote_copy(
            part_out.at[i, j - 1], part_in.at[i, j - 1], part_send.at[i, j - 1], part_recv.at[i, j - 1],
            device_id=(b, 2 * ((g + j) % ngrp) + c), device_id_type=MESH)

    def multiply(i):
        slot, k = item(i)

        @pl.when(has(slot))
        def _():
            forward_in(slot, k).wait_recv()

            def rows(group):
                return jnp.dot(
                    turned[c, group], right[slot, c, k], preferred_element_type=jnp.float32
                ) + jnp.dot(left_in[group], right[slot, 1 - c, k], preferred_element_type=jnp.float32)

            for j in range(1, ngrp):
                part_out[i, j - 1] = rows((g + j) % ngrp)
                partial(i, j).start()
            acc[i] = rows(g)

    for group in range(ngrp):
        mate_left(group).wait_recv()

    def step(i, carry):
        @pl.when(i + 1 < nitems)
        def _():
            receive(i + 1)
        multiply(i)
        return carry

    lax.fori_loop(0, nitems, step, 0)

    def store(i):
        slot, k = item(i)
        column = (offset_of(slot, e) + 2) * width + k * CHUNK
        return pltpu.make_async_copy(acc.at[i], out_ref.at[:, pl.ds(pl.multiple_of(column, CHUNK), CHUNK)], out_sem.at[i])

    def finish(i, carry):
        slot, k = item(i)

        @pl.when(has(slot))
        def _():
            total = acc[i]
            for j in range(1, ngrp):
                partial(i, j).wait_recv()
                total = total + part_in[i, j - 1]
            offset = offset_of(slot, e)
            kept = jnp.abs(offset) <= jnp.minimum(band_ref[b], band_ref[b + offset])
            acc[i] = total * jnp.where(kept, 1.0, 0.0).astype(jnp.float32)

        @pl.when(jnp.logical_not(has(slot)))
        def _():
            acc[i] = jnp.zeros(acc.shape[1:], acc.dtype)
        store(i).start()
        return carry

    lax.fori_loop(0, nitems, finish, 0)

    def drain(i, carry):
        slot, k = item(i)
        store(i).wait()

        @pl.when(has(slot))
        def _():
            forward(slot, k).wait_send()
            for j in range(1, ngrp):
                partial(i, j).wait_send()
        return carry

    lax.fori_loop(0, nitems, drain, 0)
    for group in range(ngrp):
        mate_left(group).wait_send()
    for j in range(1, nsamp):
        for k in range(nk):
            tell(j, k).wait_send()
    for k in range(nk):
        for way in (1, 2, 3):
            target, copy = direct(way, k)

            @pl.when(inside(target))
            def _():
                copy.wait_send()

        @pl.when(has(2))
        def _():
            relay(2, b - e, k).wait_send()


def on_device(nblk, nsamp, dosage, observed, band):
    depth, width = dosage.shape
    nk = width // CHUNK
    ngrp = nsamp // 2
    rows = width // nsamp
    nitems = 5 * nk
    dma = pltpu.SemaphoreType.DMA
    return pl.pallas_call(
        functools.partial(linkage_kernel, nblk, nsamp, nk),
        out_shape=jax.ShapeDtypeStruct((rows, 5 * width), jnp.float32),
        in_specs=[
            pl.BlockSpec(memory_space=pltpu.SMEM),
            pl.BlockSpec(memory_space=pl.ANY),
            pl.BlockSpec(memory_space=pl.ANY),
        ],
        out_specs=pl.BlockSpec(memory_space=pl.ANY),
        scratch_shapes=[
            pltpu.VMEM((nk, depth, CHUNK), jnp.bfloat16),
            pltpu.VMEM((nk, depth, CHUNK), jnp.int32),
            pltpu.VMEM((nsamp, nk, 8, CHUNK), jnp.float32),
            pltpu.VMEM((5, 2, nk, depth, CHUNK), jnp.bfloat16),
            pltpu.VMEM((2, ngrp, rows, depth), jnp.bfloat16),
            pltpu.VMEM((ngrp, rows, depth), jnp.bfloat16),
            pltpu.VMEM((nitems, rows, CHUNK), jnp.float32),
            pltpu.VMEM((nitems, ngrp - 1, rows, CHUNK), jnp.float32),
            pltpu.VMEM((nitems, ngrp - 1, rows, CHUNK), jnp.float32),
            dma((nk,)),
            dma((nk,)),
            dma((nsamp - 1, nk)),
            dma((nsamp - 1, nk)),
            dma((nitems,)),
            dma((4, nk)),
            dma((5, nk)),
            dma((5, nk)),
            dma((5, nk)),
            dma((nk,)),
            dma((ngrp,)),
            dma((ngrp,)),
            dma((nitems, ngrp - 1)),
            dma((nitems, ngrp - 1)),
        ],
        compiler_params=pltpu.CompilerParams(
            collective_id=0, has_side_effects=True, vmem_limit_bytes=60 * 1024 * 1024
        ),
    )(band, dosage, observed)


def solution(mesh):
    return jax.shard_map(
        functools.partial(on_device, mesh.shape["snp"], mesh.shape["samp"]),
        mesh=mesh,
        in_specs=(P("samp", "snp"), P("samp", "snp"), P()),
        out_specs=P(("snp", "samp"), None),
        check_vma=False,
    )
```
